32 devices in a mesh: row: 4 (over x, core), col: 8 (over z, y).
Axes of the slice: x: 2, y: 2, z: 4, core: 2. Of those that a mesh axis runs over, the one named last changes fastest.
Arguments:
- left_factor: bfloat16 [128, 32, 2048], P('col', None, 'row'), may hold values from -6 to 6
- right_factor: bfloat16 [128, 32, 2048], P('row', None, 'col'), may hold values from -6 to 6
- pair_grad: bfloat16 [2048, 128, 2048], P('row', None, 'col'), may hold values from -6 to 6
- projection: bfloat16 [1024, 128], replicated, may hold values from -0.1875 to 0.1875
Outputs:
- left_grad: float32 [128, 32, 2048], P('col', None, 'row')
- right_grad: float32 [128, 32, 2048], P('row', None, 'col')
The draws below stay inside these ranges and needn't reach their ends.
All inputs are finite; a program needn't handle non-finite values.
Results may differ from the reference program's by a relative error of at most 0.0029.
Values may be sent and summed in bfloat16 or wider, within the bound.
A program may use at most 576 MiB of HBM per device.

```python
import jax
import jax.numpy as jnp
from jax import lax

C = 32
CZ = 128
NRES = 2048
SEQS = 128


def level_of(key, extent, split, least, high):
    def one(position, shards_of):
        steps = jax.random.uniform(jax.random.fold_in(jax.random.fold_in(key, 6), position), (shards_of,), jnp.float32, least / len(split), high / len(split))
        return jnp.repeat(jnp.exp(steps), extent[position] // shards_of).reshape((-1,) + (1,) * (len(extent) - position - 1))

    level = one(*split[0])
    for cut in split[1:]:
        level = level * one(*cut)
    return level


def normal_values(stream_key, extent, deviation, bound, shards=(), dtype=jnp.bfloat16):
    loudness = level_of(stream_key, extent, shards, -0.22, 0.18) if shards else 1.0
    drawn = jax.random.normal(stream_key, extent, jnp.float32) * deviation * loudness
    return jnp.minimum(jnp.maximum(drawn, -bound), bound).astype(dtype)


def setup_inputs(seed: int = 0) -> dict:
    key_of = jax.random.split(jax.random.key(seed), 5)
    left_factor = normal_values(key_of[0], (SEQS, C, NRES), 1.0, 6.0, ((0, 8), (2, 4)))
    right_factor = normal_values(key_of[1], (SEQS, C, NRES), 1.0, 6.0, ((0, 4), (2, 8)))
    pair_grad = normal_values(key_of[2], (NRES, CZ, NRES), 1.0, 6.0, ((0, 4), (2, 8)))
    projection = normal_values(key_of[3], (C * C, CZ), (C * C) ** -0.5, 0.1875)
    return {"left_factor": left_factor, "right_factor": right_factor, "pair_grad": pair_grad, "projection": projection}


def reference(left_factor, right_factor, pair_grad, projection):
    total = pair_grad.shape[0]
    height = 32
    counted = total // height
    inverse = 1.0 / SEQS
    left_wide = left_factor.astype(jnp.float32)
    right_wide = right_factor.astype(jnp.float32)

    def advance(right_sum, offset):
        slab = lax.dynamic_slice_in_dim(pair_grad, offset, height, 0)
        slab = jnp.moveaxis(slab, 1, 2)
        expanded = jnp.dot(slab.reshape(height * total, CZ), projection.T, preferred_element_type=jnp.float32)
        expanded = expanded.astype(jnp.bfloat16).astype(jnp.float32).reshape(height, total, C, C)
        left_piece = jnp.einsum("ijce,sej->sci", expanded, right_wide) * inverse
        left_slab = lax.dynamic_slice_in_dim(left_wide, offset, height, 2)
        right_sum = right_sum + jnp.einsum("ijce,sci->sej", expanded, left_slab)
        return right_sum, left_piece

    offsets = (jnp.arange(counted) * height).astype(jnp.int32)
    right_sum, left_pieces = lax.scan(advance, jnp.zeros((SEQS, C, total), jnp.float32), offsets)
    left_grad = jnp.moveaxis(left_pieces, 0, 2).reshape(SEQS, C, total)
    right_grad = right_sum * inverse
    return left_grad, right_grad
```

```python
import functools

import jax
import jax.numpy as jnp
from jax import lax
from jax.experimental import pallas as pl
from jax.experimental.pallas import tpu as pltpu
from jax.sharding import PartitionSpec as P

CHUNKS = 4
BLOCK_ROWS = 16


def contract_block(channels, cols, inverse, proj_ref, grad_ref, left_ref, right_ref, before_ref, out_left_ref, sum_ref, held):
    rows = grad_ref.shape[0]

    @pl.when(pl.program_id(0) == 0)
    def _():
        sum_ref[...] = before_ref[...]

    @pl.loop(0, rows)
    def _(i):
        wide = jnp.dot(proj_ref[...], grad_ref[i], preferred_element_type=jnp.float32)
        wide = wide.astype(jnp.bfloat16)
        at = pl.ds(pl.multiple_of(i * channels, channels), channels)
        for e in range(channels):
            held[at, e * cols : (e + 1) * cols] = wide[e * channels : (e + 1) * channels]

    total = channels * cols
    step = min(1024, total)
    out_left_ref[...] = jnp.zeros_like(out_left_ref)

    @pl.loop(0, total // step)
    def _(n):
        at = pl.ds(pl.multiple_of(n * step, step), step)
        part = held[:, at]
        sum_ref[:, at] += jnp.dot(left_ref[...], part, preferred_element_type=jnp.float32)
        out_left_ref[...] += lax.dot_general(
            right_ref[:, at], part, (((1,), (1,)), ((), ())), preferred_element_type=jnp.float32
        )

    out_left_ref[...] *= inverse


def contract(proj, grad, left, right, before, chunk, chunks):
    tile_rows, width, cols = grad.shape
    sequences = left.shape[0]
    rows = tile_rows // chunks
    channels = left.shape[1] // rows
    block = min(BLOCK_ROWS, rows)
    steps = rows // block
    flops = 2 * rows * cols * channels * channels * (width + 2 * sequences)
    whole = lambda shape: pl.BlockSpec(shape, lambda n: (0, 0))
    return pl.pallas_call(
        functools.partial(contract_block, channels, cols, 1.0 / sequences),
        grid=(steps,),
        in_specs=[
            whole(proj.shape),
            pl.BlockSpec((block, width, cols), lambda n: (chunk * steps + n, 0, 0)),
            pl.BlockSpec((sequences, block * channels), lambda n: (0, n)),
            whole(right.shape),
            whole(before.shape),
        ],
        out_specs=[
            pl.BlockSpec((sequences, block * channels), lambda n: (0, n)),
            whole(before.shape),
        ],
        out_shape=[
            jax.ShapeDtypeStruct((sequences, rows * channels), jnp.float32),
            jax.ShapeDtypeStruct(before.shape, jnp.float32),
        ],
        scratch_shapes=[pltpu.VMEM((block * channels, channels * cols), jnp.bfloat16)],
        input_output_aliases={4: 1},
        compiler_params=pltpu.CompilerParams(
            dimension_semantics=("arbitrary",), vmem_limit_bytes=56 * 1024 * 1024
        ),
        cost_estimate=pl.CostEstimate(
            flops=flops, bytes_accessed=rows * width * cols * 2 + before.size * 8, transcendentals=0
        ),
    )(proj, grad, left, right, before)


def on_device(left_factor, right_factor, pair_grad, projection):
    tile_rows, width, cols = pair_grad.shape
    own, channels, _ = left_factor.shape
    right_own = right_factor.shape[0]
    proj = projection.reshape(channels, channels, width).transpose(1, 0, 2).reshape(channels * channels, width)
    right = lax.all_gather(right_factor.reshape(right_own, channels * cols), "row", axis=0, tiled=True)
    sequences = right.shape[0]
    left_own = jnp.transpose(left_factor, (0, 2, 1)).reshape(own, tile_rows * channels)
    per = tile_rows * channels // CHUNKS
    lefts = [
        lax.all_gather(left_own[:, n * per : (n + 1) * per], "col", axis=0, tiled=True) for n in range(CHUNKS)
    ]
    summed = jnp.zeros((sequences, channels * cols), jnp.float32)
    pieces = []
    for n in range(CHUNKS):
        part, summed = contract(proj, pair_grad, lefts[n], right, summed, n, CHUNKS)
        pieces.append(lax.psum_scatter(part, "col", scatter_dimension=0, tiled=True))
    right_grad = lax.psum_scatter(summed, "row", scatter_dimension=0, tiled=True)
    right_grad = right_grad.reshape(right_own, channels, cols) * (1.0 / sequences)
    left_grad = jnp.concatenate(pieces, axis=1).reshape(own, tile_rows, channels)
    return jnp.transpose(left_grad, (0, 2, 1)), right_grad


def solution(mesh):
    placed = (P("col", None, "row"), P("row", None, "col"), P("row", None, "col"), P())
    return jax.shard_map(
        on_device,
        mesh=mesh,
        in_specs=placed,
        out_specs=(P("col", None, "row"), P("row", None, "col")),
        check_vma=False,
    )
```
